32 devices in a mesh: rep: 2 (over core), row: 4 (over z), tp: 4 (over y, x).
Axes of the slice: x: 2, y: 2, z: 4, core: 2. Of those that a mesh axis runs over, the one named last changes fastest.
Arguments:
- entry_gradient: bfloat16 [2, 8, 640, 5632], P('rep', None, 'row', 'tp'), may hold values from -900 to 900
- exit_gradient: bfloat16 [2, 8, 3072, 640], P('rep', None, 'row', 'tp'), may hold values from -900 to 900
- embed_gradient: bfloat16 [2, 8192, 640], P('rep', 'row', 'tp'), may hold values from -900 to 900
- gain_gradient: bfloat16 [2, 8, 3072], P('rep'), may hold values from -900 to 900
- master: float32 [4, 4, 2, 1556480], P('tp', 'row', 'rep'), may hold values from -5 to 5
- momentum: float32 [4, 4, 2, 1556480], P('tp', 'row', 'rep'), may hold values from -4 to 4
- variance: float32 [4, 4, 2, 1556480], P('tp', 'row', 'rep'), may hold values from 0.01 to 1
- entry_average: float32 [8, 640, 5632], P(None, 'row', 'tp'), may hold values from -5 to 5
- exit_average: float32 [8, 3072, 640], P(None, 'row', 'tp'), may hold values from -5 to 5
- embed_average: float32 [8192, 640], P('row', 'tp'), may hold values from -5 to 5
- gain_master: float32 [8, 3072], replicated, may hold values from -5 to 5
- gain_momentum: float32 [8, 3072], replicated, may hold values from -4 to 4
- gain_variance: float32 [8, 3072], replicated, may hold values from 0.01 to 1
Outputs:
- next_master: float32 [4, 4, 2, 1556480], P('tp', 'row', 'rep')
- next_momentum: float32 [4, 4, 2, 1556480], P('tp', 'row', 'rep')
- next_variance: float32 [4, 4, 2, 1556480], P('tp', 'row', 'rep')
- entry_weight: bfloat16 [8, 640, 5632], P(None, 'row', 'tp')
- exit_weight: bfloat16 [8, 3072, 640], P(None, 'row', 'tp')
- embed_weight: bfloat16 [8192, 640], P('row', 'tp')
- entry_averaged: float32 [8, 640, 5632], P(None, 'row', 'tp')
- exit_averaged: float32 [8, 3072, 640], P(None, 'row', 'tp')
- embed_averaged: float32 [8192, 640], P('row', 'tp')
- fresh_gain: float32 [8, 3072], replicated
- fresh_momentum: float32 [8, 3072], replicated
- fresh_variance: float32 [8, 3072], replicated
The draws below stay inside these ranges and needn't reach their ends.
All inputs are finite; a program needn't handle non-finite values.
Results may differ from the reference program's by a relative error of at most 0.0028.
Values may be sent and summed in bfloat16 or wider, within the bound.
No kernel may reach another device: no remote copies, remote signals or barrier semaphores. Data moves between devices by JAX's collectives and lax.ppermute only.
A program may use at most 256 MiB of HBM per device.

```python
import math
import jax
import jax.numpy as jnp
from jax import lax

D = 640
VOCAB_ROWS = 8192
LAYERS = 8
IN_COLS = 5632
OUT_ROWS = 3072
NORM_LEN = 3072
PIECE = 1556480
N_REP = 2
N_ROW = 4
N_TP = 4


def rough_gradient(key, shape):
    base_key, row_key, column_key = jax.random.split(key, 3)
    height = shape[-2]
    breadth = shape[-1]
    row_factor = jnp.exp(math.log(10.0) * jax.random.uniform(row_key, (height, 1), jnp.float32))
    position = jnp.arange(breadth, dtype=jnp.float32) / breadth
    column_factor = jnp.exp(math.log(10.0) * jax.random.uniform(column_key, (breadth,), jnp.float32) + 0.5 * math.log(3.0) * position)
    values = jnp.clip(jax.random.normal(base_key, shape, jnp.float32), -5.0, 5.0)
    return (values * row_factor * column_factor).astype(jnp.bfloat16)


def draw_entry_gradient(key, part):
    return rough_gradient(jax.random.fold_in(key, 11), (N_REP, LAYERS, D, IN_COLS))


def draw_exit_gradient(key, part):
    return rough_gradient(jax.random.fold_in(key, 12), (N_REP, LAYERS, OUT_ROWS, D))


def draw_embed_gradient(key, part):
    return rough_gradient(jax.random.fold_in(key, 13), (N_REP, VOCAB_ROWS, D))


def draw_gain_gradient(key, part):
    return rough_gradient(jax.random.fold_in(key, 14), (N_REP, LAYERS, NORM_LEN))


def steps_of(stream_key, dims, pieces, least, high):
    factor_of = 1.0
    for dim, blocks in pieces:
        draws = jax.random.uniform(jax.random.fold_in(jax.random.fold_in(stream_key, 6), dim), (blocks,), jnp.float32, least / len(pieces), high / len(pieces))
        factor_of = factor_of * jnp.repeat(jnp.exp(draws), dims[dim] // blocks).reshape((-1,) + (1,) * (len(dims) - 1 - dim))
    return factor_of


def scatter_about(key, dims, spread, most, cuts=(), kind=jnp.bfloat16):
    values = jax.random.normal(key, dims, jnp.float32) * spread
    if len(cuts) > 0:
        values = steps_of(key, dims, cuts, -0.22, 0.18) * values
    return jnp.clip(values, min=-most, max=most).astype(kind)


def setup_inputs(seed: int = 0) -> dict:
    key_of = jax.random.split(jax.random.key(seed), 14)
    return {
        "entry_gradient": draw_entry_gradient(jax.random.fold_in(key_of[13], 71), 0),
        "exit_gradient": draw_exit_gradient(jax.random.fold_in(key_of[13], 71), 0),
        "embed_gradient": draw_embed_gradient(jax.random.fold_in(key_of[13], 71), 0),
        "gain_gradient": draw_gain_gradient(jax.random.fold_in(key_of[13], 71), 0),
        "master": scatter_about(key_of[4], (N_TP, N_ROW, N_REP, PIECE), 1.0, 5.0, ((0, 4), (1, 4), (2, 2)), jnp.float32),
        "momentum": scatter_about(key_of[5], (N_TP, N_ROW, N_REP, PIECE), 0.3, 4.0, ((0, 4), (1, 4), (2, 2)), jnp.float32),
        "variance": jnp.clip(jnp.exp(math.log(1.0) - 4.6051702 * jax.random.uniform(key_of[6], (N_TP, N_ROW, N_REP, PIECE), jnp.float32) ** steps_of(key_of[6], (N_TP, N_ROW, N_REP, PIECE), ((0, 4), (1, 4), (2, 2)), -0.2, 0.2)), 0.01, 1.0),
        "entry_average": scatter_about(key_of[7], (LAYERS, D, IN_COLS), 1.0, 5.0, ((1, 4), (2, 4)), jnp.float32),
        "exit_average": scatter_about(key_of[8], (LAYERS, OUT_ROWS, D), 1.0, 5.0, ((1, 4), (2, 4)), jnp.float32),
        "embed_average": scatter_about(key_of[9], (VOCAB_ROWS, D), 1.0, 5.0, ((0, 4), (1, 4)), jnp.float32),
        "gain_master": scatter_about(key_of[10], (LAYERS, NORM_LEN), 0.5, 5.0, (), jnp.float32),
        "gain_momentum": scatter_about(key_of[11], (LAYERS, NORM_LEN), 0.3, 4.0, (), jnp.float32),
        "gain_variance": jnp.clip(jnp.exp(jax.random.uniform(key_of[12], (LAYERS, NORM_LEN), jnp.float32, math.log(0.01), math.log(1.0))), 0.01, 1.0),
    }


beta_one = 0.9
beta_two = 0.95
learn_rate = 0.02
decay_rate = 0.1
epsilon = 1e-08
clip_level = 0.5
bias_one = 1.0 - 0.9 ** 20
bias_two = 1.0 - 0.95 ** 20
average_decay = 0.99

def clip_factor(square_sum):
    entries = LAYERS * (D * IN_COLS + OUT_ROWS * D + NORM_LEN) + VOCAB_ROWS * D
    return jnp.minimum(1.0, clip_level * math.sqrt(entries) / (jnp.sqrt(square_sum) + 1e-06))

def adam_update(gradient, momentum, variance, master, clip_scale):
    clipped = clip_scale * gradient
    moved_first = beta_one * momentum + (1.0 - beta_one) * clipped
    moved_second = beta_two * variance + (1.0 - beta_two) * clipped * clipped
    stepped = master * (1.0 - learn_rate * decay_rate) - learn_rate * (moved_first / bias_one) / (jnp.sqrt(moved_second / bias_two) + epsilon)
    return (stepped, moved_first, moved_second)

def to_flat(whole):
    layer_count, height, breadth = whole.shape
    half_rows = height // (N_ROW * N_REP)
    strip_width = breadth // (N_TP * N_ROW)
    arranged = whole.reshape(layer_count, N_ROW, N_REP, half_rows, N_TP, N_ROW, strip_width)
    return arranged.transpose(4, 5, 2, 0, 1, 3, 6).reshape(N_TP, N_ROW, N_REP, -1)

def from_flat(flat_part, layer_count, height, breadth):
    half_rows = height // (N_ROW * N_REP)
    strip_width = breadth // (N_TP * N_ROW)
    arranged = flat_part.reshape(N_TP, N_ROW, N_REP, layer_count, N_ROW, half_rows, strip_width)
    return arranged.transpose(3, 4, 2, 5, 0, 1, 6).reshape(layer_count, height, breadth)

def reference(entry_gradient, exit_gradient, embed_gradient, gain_gradient, master, momentum, variance, entry_average, exit_average, embed_average, gain_master, gain_momentum, gain_variance):
    entry_sum = lax.optimization_barrier(jnp.sum(entry_gradient.astype(jnp.float32), axis=0))
    exit_sum = lax.optimization_barrier(jnp.sum(exit_gradient.astype(jnp.float32), axis=0))
    embed_sum = lax.optimization_barrier(jnp.sum(embed_gradient.astype(jnp.float32), axis=0))
    gain_sum = lax.optimization_barrier(jnp.sum(gain_gradient.astype(jnp.float32), axis=0))
    flat_grad = jnp.concatenate([to_flat(entry_sum), to_flat(exit_sum), to_flat(embed_sum[None])], axis=3)
    square_sum = jnp.sum(flat_grad * flat_grad) + jnp.sum(gain_sum * gain_sum)
    clip_scale = clip_factor(square_sum)
    next_master, next_momentum, next_variance = adam_update(flat_grad, momentum, variance, master, clip_scale)
    flat_weight = next_master.astype(jnp.bfloat16)
    pieces_total = N_TP * N_ROW * N_REP
    entry_len = LAYERS * D * IN_COLS // pieces_total
    exit_len = LAYERS * OUT_ROWS * D // pieces_total
    entry_weight = from_flat(flat_weight[..., :entry_len], LAYERS, D, IN_COLS)
    exit_weight = from_flat(flat_weight[..., entry_len:entry_len + exit_len], LAYERS, OUT_ROWS, D)
    embed_weight = from_flat(flat_weight[..., entry_len + exit_len:], 1, VOCAB_ROWS, D)[0]
    entry_averaged = average_decay * entry_average + (1.0 - average_decay) * entry_weight.astype(jnp.float32)
    exit_averaged = average_decay * exit_average + (1.0 - average_decay) * exit_weight.astype(jnp.float32)
    embed_averaged = average_decay * embed_average + (1.0 - average_decay) * embed_weight.astype(jnp.float32)
    fresh_gain, fresh_momentum, fresh_variance = adam_update(gain_sum, gain_momentum, gain_variance, gain_master, clip_scale)
    return (next_master, next_momentum, next_variance, entry_weight, exit_weight, embed_weight, entry_averaged, exit_averaged, embed_averaged, fresh_gain, fresh_momentum, fresh_variance)
```

```python
import math

import jax
import jax.numpy as jnp
from jax import lax
from jax.experimental import pallas as pl
from jax.experimental.pallas import tpu as pltpu
from jax.sharding import PartitionSpec as P

D = 640
VOCAB_ROWS = 8192
LAYERS = 8
IN_COLS = 5632
OUT_ROWS = 3072
NORM_LEN = 3072


beta_one = 0.9
beta_two = 0.95
learn_rate = 0.02
decay_rate = 0.1
epsilon = 1e-08
clip_level = 0.5
bias_one = 1.0 - 0.9**20
bias_two = 1.0 - 0.95**20
average_decay = 0.99


def clip_factor(square_sum):
    entries = LAYERS * (D * IN_COLS + OUT_ROWS * D + NORM_LEN) + VOCAB_ROWS * D
    return jnp.minimum(1.0, clip_level * math.sqrt(entries) / (jnp.sqrt(square_sum) + 1e-06))


def adam_update(gradient, momentum, variance, master, clip_scale):
    clipped = clip_scale * gradient
    moved_first = beta_one * momentum + (1.0 - beta_one) * clipped
    moved_second = beta_two * variance + (1.0 - beta_two) * clipped * clipped
    stepped = master * (1.0 - learn_rate * decay_rate) - learn_rate * (moved_first / bias_one) / (
        jnp.sqrt(moved_second / bias_two) + epsilon
    )
    return (stepped, moved_first, moved_second)


LANES = 128
TILE_ROWS = 640


def swap(moving, axis, distance):
    count = lax.axis_size(axis)
    return lax.ppermute(moving, axis, [(i, i ^ distance) for i in range(count)])


def all_sum(value, axis):
    count = lax.axis_size(axis)
    step = 1
    while step < count:
        if step * 2 < count:
            one = swap(value, axis, step)
            two = swap(value, axis, step * 2)
            three = swap(value, axis, step * 3)
            value = (value + one) + (two + three)
            step = step * 4
        else:
            value = value + swap(value, axis, step)
            step = step * 2
    return value


def half_sum(matrix_block):
    half = matrix_block.shape[1] // lax.axis_size("rep")
    mine = lax.axis_index("rep")
    kept = lax.dynamic_slice_in_dim(matrix_block, mine * half, half, 1)
    sent = lax.dynamic_slice_in_dim(matrix_block, (1 - mine) * half, half, 1)
    arrived = swap(sent, "rep", 1)
    return (kept.astype(jnp.float32) + arrived.astype(jnp.float32)).astype(jnp.bfloat16)


def both_halves(half):
    other = swap(half, "rep", 1)
    first = lax.axis_index("rep") == 0
    return jnp.concatenate(
        [jnp.where(first, half, other), jnp.where(first, other, half)], axis=1
    )


def to_owner(part, row_count):
    layer_count, half, block_cols = part.shape
    arrived = lax.all_to_all(part, "row", split_axis=2, concat_axis=1, tiled=True)
    return arrived.reshape(-1, LANES)


def to_holder(section, row_count):
    layer_count, row_count, half, width = section.shape
    block = lax.all_to_all(section, "row", split_axis=1, concat_axis=3, tiled=True)
    return block.reshape(layer_count, half, width * row_count)


def update_body(scale_ref, gradient_ref, momentum_ref, variance_ref, master_ref, *refs):
    master_out, momentum_out, variance_out, weight_out = refs[-4:]
    stepped, moved_first, moved_second = adam_update(
        gradient_ref[...].astype(jnp.float32),
        momentum_ref[...],
        variance_ref[...],
        master_ref[...],
        scale_ref[0, 0],
    )
    master_out[...] = stepped
    momentum_out[...] = moved_first
    variance_out[...] = moved_second
    weight_out[...] = stepped.astype(jnp.bfloat16)


def update_section(scale, gradient, momentum, variance, master, start, carried):
    rows = gradient.shape[0]
    tile = math.gcd(math.gcd(rows, start), TILE_ROWS)
    first = start // tile
    here = pl.BlockSpec((tile, LANES), lambda i: (i, 0))
    there = pl.BlockSpec((tile, LANES), lambda i: (i + first, 0))
    whole = jax.ShapeDtypeStruct(master.shape, jnp.float32)
    extra = [] if carried is None else list(carried)
    return pl.pallas_call(
        update_body,
        grid=(rows // tile,),
        in_specs=[pl.BlockSpec(memory_space=pltpu.SMEM), here, there, there, there]
        + [pl.BlockSpec(memory_space=pl.ANY) for _ in extra],
        out_specs=[there, there, there, here],
        out_shape=[whole, whole, whole, jax.ShapeDtypeStruct(gradient.shape, jnp.bfloat16)],
        input_output_aliases={5 + k: k for k in range(len(extra))},
        name="update",
    )(scale, gradient, momentum, variance, master, *extra)


def shards(
    entry_gradient,
    exit_gradient,
    embed_gradient,
    gain_gradient,
    master,
    momentum,
    variance,
    entry_average,
    exit_average,
    embed_average,
    gain_master,
    gain_momentum,
    gain_variance,
):
    row_count = lax.axis_size("row")
    matrices = [entry_gradient[0], exit_gradient[0], embed_gradient[0][None]]
    averages = [entry_average, exit_average, embed_average[None]]
    gain_local = gain_gradient[0]
    gain_total = gain_local.astype(jnp.float32) + swap(gain_local, "rep", 1).astype(jnp.float32)
    gain_total = gain_total.astype(jnp.bfloat16).astype(jnp.float32)
    sums = [half_sum(matrix_block) for matrix_block in matrices]
    local_squares = sum(jnp.sum(jnp.square(part.astype(jnp.float32))) for part in sums)
    local_squares = local_squares.reshape(1, 1)
    for axis in ("rep", "row", "tp"):
        local_squares = all_sum(local_squares, axis)
    clip_scale = clip_factor(local_squares + jnp.sum(gain_total * gain_total))

    flat = [array.reshape(-1, LANES) for array in (momentum, variance, master)]
    carried = None
    start = 0
    order = (0, 1, 2)
    starts = []
    for part in sums:
        starts.append(start)
        start = start + part.size // LANES
    weights = [None] * len(sums)
    averaged = [None] * len(sums)
    for k in order:
        part = sums[k]
        layer_count, half, block_cols = part.shape
        width = block_cols // row_count
        arrived = to_owner(part, row_count)
        *carried, weight = update_section(
            clip_scale, arrived, *flat, starts[k], carried
        )
        section = weight.reshape(layer_count, row_count, half, width)
        block = to_holder(section, row_count)
        weights[k] = both_halves(block)
        averaged[k] = average_decay * averages[k] + (1.0 - average_decay) * weights[k].astype(
            jnp.float32
        )
    fresh_gain, fresh_momentum, fresh_variance = adam_update(
        gain_total, gain_momentum, gain_variance, gain_master, clip_scale
    )
    next_master, next_momentum, next_variance = [array.reshape(master.shape) for array in carried]
    return (
        next_master,
        next_momentum,
        next_variance,
        weights[0],
        weights[1],
        weights[2][0],
        averaged[0],
        averaged[1],
        averaged[2][0],
        fresh_gain,
        fresh_momentum,
        fresh_variance,
    )


def solution(mesh):
    placed = (
        P("rep", None, "row", "tp"),
        P("rep", None, "row", "tp"),
        P("rep", "row", "tp"),
        P("rep", None, None),
        P("tp", "row", "rep", None),
        P("tp", "row", "rep", None),
        P("tp", "row", "rep", None),
        P(None, "row", "tp"),
        P(None, "row", "tp"),
        P("row", "tp"),
        P(),
        P(),
        P(),
    )
    return jax.shard_map(
        shards,
        mesh=mesh,
        in_specs=placed,
        out_specs=(
            P("tp", "row", "rep", None),
            P("tp", "row", "rep", None),
            P("tp", "row", "rep", None),
            P(None, "row", "tp"),
            P(None, "row", "tp"),
            P("row", "tp"),
            P(None, "row", "tp"),
            P(None, "row", "tp"),
            P("row", "tp"),
            P(),
            P(),
            P(),
        ),
        check_vma=False,
    )
```

```python
import math

import jax
import jax.numpy as jnp
from jax import lax
from jax.experimental import pallas as pl
from jax.experimental.pallas import tpu as pltpu
from jax.sharding import PartitionSpec as P

D = 640
VOCAB_ROWS = 8192
LAYERS = 8
IN_COLS = 5632
OUT_ROWS = 3072
NORM_LEN = 3072


beta_one = 0.9
beta_two = 0.95
learn_rate = 0.02
decay_rate = 0.1
epsilon = 1e-08
clip_level = 0.5
bias_one = 1.0 - 0.9**20
bias_two = 1.0 - 0.95**20
average_decay = 0.99


def clip_factor(square_sum):
    entries = LAYERS * (D * IN_COLS + OUT_ROWS * D + NORM_LEN) + VOCAB_ROWS * D
    return jnp.minimum(1.0, clip_level * math.sqrt(entries) / (jnp.sqrt(square_sum) + 1e-06))


def adam_update(gradient, momentum, variance, master, clip_scale):
    clipped = clip_scale * gradient
    moved_first = beta_one * momentum + (1.0 - beta_one) * clipped
    moved_second = beta_two * variance + (1.0 - beta_two) * clipped * clipped
    stepped = master * (1.0 - learn_rate * decay_rate) - learn_rate * (moved_first / bias_one) / (
        jnp.sqrt(moved_second / bias_two) + epsilon
    )
    return (stepped, moved_first, moved_second)


LANES = 128
TILE_ROWS = 640


def swap(moving, axis, distance):
    count = lax.axis_size(axis)
    return lax.ppermute(moving, axis, [(i, i ^ distance) for i in range(count)])


def all_sum(value, axis):
    count = lax.axis_size(axis)
    step = 1
    while step < count:
        if step * 2 < count:
            one = swap(value, axis, step)
            two = swap(value, axis, step * 2)
            three = swap(value, axis, step * 3)
            value = (value + one) + (two + three)
            step = step * 4
        else:
            value = value + swap(value, axis, step)
            step = step * 2
    return value


def after(value, *earlier):
    return lax.optimization_barrier((value, *earlier))[0]


def half_sum(matrix_block):
    half = matrix_block.shape[1] // lax.axis_size("rep")
    mine = lax.axis_index("rep")
    kept = lax.dynamic_slice_in_dim(matrix_block, mine * half, half, 1)
    sent = lax.dynamic_slice_in_dim(matrix_block, (1 - mine) * half, half, 1)
    arrived = swap(sent, "rep", 1)
    return (kept.astype(jnp.float32) + arrived.astype(jnp.float32)).astype(jnp.bfloat16)


def both_halves(half):
    other = swap(half, "rep", 1)
    first = lax.axis_index("rep") == 0
    return jnp.concatenate(
        [jnp.where(first, half, other), jnp.where(first, other, half)], axis=1
    )


def to_owner(part, row_count):
    layer_count, half, block_cols = part.shape
    if half % LANES == 0:
        arrived = lax.all_to_all(part, "row", split_axis=2, concat_axis=1, tiled=True)
    else:
        pieces = part.reshape(layer_count, half, row_count, -1).transpose(0, 2, 1, 3)
        arrived = lax.all_to_all(pieces, "row", split_axis=1, concat_axis=1, tiled=True)
    return arrived.reshape(-1, LANES)


def to_holder(section, row_count):
    layer_count, row_count, half, width = section.shape
    block = lax.all_to_all(section, "row", split_axis=1, concat_axis=3, tiled=True)
    return block.reshape(layer_count, half, width * row_count)


def update_body(scale_ref, gradient_ref, momentum_ref, variance_ref, master_ref, *refs):
    master_out, momentum_out, variance_out, weight_out = refs[-4:]
    stepped, moved_first, moved_second = adam_update(
        gradient_ref[...].astype(jnp.float32),
        momentum_ref[...],
        variance_ref[...],
        master_ref[...],
        scale_ref[0, 0],
    )
    master_out[...] = stepped
    momentum_out[...] = moved_first
    variance_out[...] = moved_second
    weight_out[...] = stepped.astype(jnp.bfloat16)


def update_section(scale, gradient, momentum, variance, master, start, carried):
    rows = gradient.shape[0]
    tile = math.gcd(math.gcd(rows, start), TILE_ROWS)
    first = start // tile
    here = pl.BlockSpec((tile, LANES), lambda i: (i, 0))
    there = pl.BlockSpec((tile, LANES), lambda i: (i + first, 0))
    whole = jax.ShapeDtypeStruct(master.shape, jnp.float32)
    extra = [] if carried is None else list(carried)
    return pl.pallas_call(
        update_body,
        grid=(rows // tile,),
        in_specs=[pl.BlockSpec(memory_space=pltpu.SMEM), here, there, there, there]
        + [pl.BlockSpec(memory_space=pl.ANY) for _ in extra],
        out_specs=[there, there, there, here],
        out_shape=[whole, whole, whole, jax.ShapeDtypeStruct(gradient.shape, jnp.bfloat16)],
        input_output_aliases={5 + k: k for k in range(len(extra))},
        name="update",
    )(scale, gradient, momentum, variance, master, *extra)


def shards(
    entry_gradient,
    exit_gradient,
    embed_gradient,
    gain_gradient,
    master,
    momentum,
    variance,
    entry_average,
    exit_average,
    embed_average,
    gain_master,
    gain_momentum,
    gain_variance,
):
    row_count = lax.axis_size("row")
    matrices = [entry_gradient[0], exit_gradient[0], embed_gradient[0][None]]
    averages = [entry_average, exit_average, embed_average[None]]
    gain_local = gain_gradient[0]
    gain_total = gain_local.astype(jnp.float32) + swap(gain_local, "rep", 1).astype(jnp.float32)
    gain_total = gain_total.astype(jnp.bfloat16).astype(jnp.float32)
    sums = [half_sum(matrix_block) for matrix_block in matrices]
    local_squares = sum(jnp.sum(jnp.square(part.astype(jnp.float32))) for part in sums)
    local_squares = local_squares.reshape(1, 1)
    for axis in ("rep", "tp", "row"):
        local_squares = all_sum(local_squares, axis)
    clip_scale = clip_factor(local_squares + jnp.sum(gain_total * gain_total))

    flat = [array.reshape(-1, LANES) for array in (momentum, variance, master)]
    starts = [0, sums[0].size // LANES, (sums[0].size + sums[1].size) // LANES]
    arrived = [None] * 3
    arrived[2] = to_owner(sums[2], row_count)
    arrived[1] = to_owner(after(sums[1], arrived[2]), row_count)
    arrived[0] = to_owner(after(sums[0], arrived[1], clip_scale), row_count)
    carried = None
    updated = [None] * 3
    for k in (2, 1, 0):
        layer_count, half, block_cols = sums[k].shape
        *carried, weight = update_section(
            clip_scale, arrived[k], *flat, starts[k], carried
        )
        updated[k] = weight.reshape(layer_count, row_count, half, block_cols // row_count)
    blocks = [None] * 3
    blocks[1] = to_holder(after(updated[1], arrived[0]), row_count)
    blocks[0] = to_holder(after(updated[0], blocks[1]), row_count)
    blocks[2] = to_holder(after(updated[2], blocks[0]), row_count)
    weights = [both_halves(block) for block in blocks]
    averaged = [
        average_decay * average + (1.0 - average_decay) * weight.astype(jnp.float32)
        for average, weight in zip(averages, weights)
    ]
    fresh_gain, fresh_momentum, fresh_variance = adam_update(
        gain_total, gain_momentum, gain_variance, gain_master, clip_scale
    )
    next_master, next_momentum, next_variance = [array.reshape(master.shape) for array in carried]
    return (
        next_master,
        next_momentum,
        next_variance,
        weights[0],
        weights[1],
        weights[2][0],
        averaged[0],
        averaged[1],
        averaged[2][0],
        fresh_gain,
        fresh_momentum,
        fresh_variance,
    )


def solution(mesh):
    placed = (
        P("rep", None, "row", "tp"),
        P("rep", None, "row", "tp"),
        P("rep", "row", "tp"),
        P("rep", None, None),
        P("tp", "row", "rep", None),
        P("tp", "row", "rep", None),
        P("tp", "row", "rep", None),
        P(None, "row", "tp"),
        P(None, "row", "tp"),
        P("row", "tp"),
        P(),
        P(),
        P(),
    )
    return jax.shard_map(
        shards,
        mesh=mesh,
        in_specs=placed,
        out_specs=(
            P("tp", "row", "rep", None),
            P("tp", "row", "rep", None),
            P("tp", "row", "rep", None),
            P(None, "row", "tp"),
            P(None, "row", "tp"),
            P("row", "tp"),
            P(None, "row", "tp"),
            P(None, "row", "tp"),
            P("row", "tp"),
            P(),
            P(),
            P(),
        ),
        check_vma=False,
    )
```

```python
import math

import jax
import jax.numpy as jnp
from jax import lax
from jax.experimental import pallas as pl
from jax.experimental.pallas import tpu as pltpu
from jax.sharding import PartitionSpec as P

D = 640
VOCAB_ROWS = 8192
LAYERS = 8
IN_COLS = 5632
OUT_ROWS = 3072
NORM_LEN = 3072


beta_one = 0.9
beta_two = 0.95
learn_rate = 0.02
decay_rate = 0.1
epsilon = 1e-08
clip_level = 0.5
bias_one = 1.0 - 0.9**20
bias_two = 1.0 - 0.95**20
average_decay = 0.99


def clip_factor(square_sum):
    entries = LAYERS * (D * IN_COLS + OUT_ROWS * D + NORM_LEN) + VOCAB_ROWS * D
    return jnp.minimum(1.0, clip_level * math.sqrt(entries) / (jnp.sqrt(square_sum) + 1e-06))


def adam_update(gradient, momentum, variance, master, clip_scale):
    clipped = clip_scale * gradient
    moved_first = beta_one * momentum + (1.0 - beta_one) * clipped
    moved_second = beta_two * variance + (1.0 - beta_two) * clipped * clipped
    stepped = master * (1.0 - learn_rate * decay_rate) - learn_rate * (moved_first / bias_one) / (
        jnp.sqrt(moved_second / bias_two) + epsilon
    )
    return (stepped, moved_first, moved_second)


LANES = 128
TILE_ROWS = 640


def swap(moving, axis, distance):
    count = lax.axis_size(axis)
    return lax.ppermute(moving, axis, [(i, i ^ distance) for i in range(count)])


def all_sum(value, axis):
    count = lax.axis_size(axis)
    step = 1
    while step < count:
        if step * 2 < count:
            one = swap(value, axis, step)
            two = swap(value, axis, step * 2)
            three = swap(value, axis, step * 3)
            value = (value + one) + (two + three)
            step = step * 4
        else:
            value = value + swap(value, axis, step)
            step = step * 2
    return value


def after(value, *earlier):
    return lax.optimization_barrier((value, *earlier))[0]


def half_sum(matrix_block):
    half = matrix_block.shape[1] // lax.axis_size("rep")
    mine = lax.axis_index("rep")
    kept = lax.dynamic_slice_in_dim(matrix_block, mine * half, half, 1)
    sent = lax.dynamic_slice_in_dim(matrix_block, (1 - mine) * half, half, 1)
    arrived = swap(sent, "rep", 1)
    return (kept.astype(jnp.float32) + arrived.astype(jnp.float32)).astype(jnp.bfloat16)


def both_halves(half):
    other = swap(half, "rep", 1)
    first = lax.axis_index("rep") == 0
    return jnp.concatenate(
        [jnp.where(first, half, other), jnp.where(first, other, half)], axis=1
    )


def move(pieces):
    return lax.all_to_all(pieces, "row", split_axis=0, concat_axis=0, tiled=True)


def owner_pieces(part, row_count, narrow):
    layer_count, half, block_cols = part.shape
    split = part.reshape(layer_count, half, row_count, -1)
    if narrow:
        return split.transpose(2, 0, 3, 1)
    return split.transpose(2, 0, 1, 3)


def owner_rows(arrived, narrow):
    if narrow:
        arrived = arrived.transpose(1, 0, 3, 2)
    else:
        arrived = arrived.transpose(1, 0, 2, 3)
    return arrived.reshape(-1, LANES)


def holder_pieces(section, narrow):
    if narrow:
        return section.transpose(1, 0, 3, 2)
    return section.transpose(1, 0, 2, 3)


def holder_block(arrived, narrow):
    if narrow:
        block = arrived.transpose(1, 3, 0, 2)
    else:
        block = arrived.transpose(1, 2, 0, 3)
    return block.reshape(*block.shape[:2], -1)


def update_body(scale_ref, gradient_ref, momentum_ref, variance_ref, master_ref, *refs):
    master_out, momentum_out, variance_out, weight_out = refs[-4:]
    stepped, moved_first, moved_second = adam_update(
        gradient_ref[...].astype(jnp.float32),
        momentum_ref[...],
        variance_ref[...],
        master_ref[...],
        scale_ref[0, 0],
    )
    master_out[...] = stepped
    momentum_out[...] = moved_first
    variance_out[...] = moved_second
    weight_out[...] = stepped.astype(jnp.bfloat16)


def update_section(scale, gradient, momentum, variance, master, start, carried):
    rows = gradient.shape[0]
    tile = math.gcd(math.gcd(rows, start), TILE_ROWS)
    first = start // tile
    here = pl.BlockSpec((tile, LANES), lambda i: (i, 0))
    there = pl.BlockSpec((tile, LANES), lambda i: (i + first, 0))
    whole = jax.ShapeDtypeStruct(master.shape, jnp.float32)
    extra = [] if carried is None else list(carried)
    return pl.pallas_call(
        update_body,
        grid=(rows // tile,),
        in_specs=[pl.BlockSpec(memory_space=pltpu.SMEM), here, there, there, there]
        + [pl.BlockSpec(memory_space=pl.ANY) for _ in extra],
        out_specs=[there, there, there, here],
        out_shape=[whole, whole, whole, jax.ShapeDtypeStruct(gradient.shape, jnp.bfloat16)],
        input_output_aliases={5 + k: k for k in range(len(extra))},
        name="update",
    )(scale, gradient, momentum, variance, master, *extra)


def shards(
    entry_gradient,
    exit_gradient,
    embed_gradient,
    gain_gradient,
    master,
    momentum,
    variance,
    entry_average,
    exit_average,
    embed_average,
    gain_master,
    gain_momentum,
    gain_variance,
):
    row_count = lax.axis_size("row")
    matrices = [entry_gradient[0], exit_gradient[0], embed_gradient[0][None]]
    averages = [entry_average, exit_average, embed_average[None]]
    gain_local = gain_gradient[0]
    gain_total = gain_local.astype(jnp.float32) + swap(gain_local, "rep", 1).astype(jnp.float32)
    gain_total = gain_total.astype(jnp.bfloat16).astype(jnp.float32)
    sums = [half_sum(matrix_block) for matrix_block in matrices]
    local_squares = sum(jnp.sum(jnp.square(part.astype(jnp.float32))) for part in sums)
    local_squares = local_squares.reshape(1, 1)
    row_squares = all_sum(all_sum(local_squares, "rep"), "row")
    clip_scale = clip_factor(all_sum(row_squares, "tp") + jnp.sum(gain_total * gain_total))

    flat = [array.reshape(-1, LANES) for array in (momentum, variance, master)]
    starts = [0, sums[0].size // LANES, (sums[0].size + sums[1].size) // LANES]
    narrow = [part.shape[2] < part.shape[1] for part in sums]
    pieces = [
        owner_pieces(part, row_count, thin) for part, thin in zip(sums, narrow)
    ]
    moved = [None] * 3
    moved[2] = move(pieces[2])
    moved[1] = move(after(pieces[1], moved[2]))
    moved[0] = move(after(pieces[0], moved[1], row_squares))
    carried = None
    pieces = [None] * 3
    for k in (2, 1, 0):
        layer_count, half, block_cols = sums[k].shape
        arrived = moved[k] if k == 0 else after(moved[k], clip_scale)
        *carried, weight = update_section(
            clip_scale, owner_rows(arrived, narrow[k]), *flat, starts[k], carried
        )
        pieces[k] = holder_pieces(
            weight.reshape(layer_count, row_count, half, block_cols // row_count), narrow[k]
        )
    back = [None] * 3
    weights = [None] * 3
    averaged = [None] * 3

    def settle(k):
        weights[k] = both_halves(holder_block(back[k], narrow[k]))
        averaged[k] = average_decay * averages[k] + (1.0 - average_decay) * weights[k].astype(
            jnp.float32
        )

    back[1] = move(after(pieces[1], moved[0]))
    settle(1)
    back[0] = move(after(pieces[0], back[1]))
    back[2] = move(after(pieces[2], back[0], averaged[1]))
    settle(0)
    settle(2)
    fresh_gain, fresh_momentum, fresh_variance = adam_update(
        gain_total, gain_momentum, gain_variance, gain_master, clip_scale
    )
    next_master, next_momentum, next_variance = [array.reshape(master.shape) for array in carried]
    return (
        next_master,
        next_momentum,
        next_variance,
        weights[0],
        weights[1],
        weights[2][0],
        averaged[0],
        averaged[1],
        averaged[2][0],
        fresh_gain,
        fresh_momentum,
        fresh_variance,
    )


def solution(mesh):
    placed = (
        P("rep", None, "row", "tp"),
        P("rep", None, "row", "tp"),
        P("rep", "row", "tp"),
        P("rep", None, None),
        P("tp", "row", "rep", None),
        P("tp", "row", "rep", None),
        P("tp", "row", "rep", None),
        P(None, "row", "tp"),
        P(None, "row", "tp"),
        P("row", "tp"),
        P(),
        P(),
        P(),
    )
    return jax.shard_map(
        shards,
        mesh=mesh,
        in_specs=placed,
        out_specs=(
            P("tp", "row", "rep", None),
            P("tp", "row", "rep", None),
            P("tp", "row", "rep", None),
            P(None, "row", "tp"),
            P(None, "row", "tp"),
            P("row", "tp"),
            P(None, "row", "tp"),
            P(None, "row", "tp"),
            P("row", "tp"),
            P(),
            P(),
            P(),
        ),
        check_vma=False,
    )
```

```python
import math

import jax
import jax.numpy as jnp
from jax import lax
from jax.experimental import pallas as pl
from jax.experimental.pallas import tpu as pltpu
from jax.sharding import PartitionSpec as P

D = 640
VOCAB_ROWS = 8192
LAYERS = 8
IN_COLS = 5632
OUT_ROWS = 3072
NORM_LEN = 3072


beta_one = 0.9
beta_two = 0.95
learn_rate = 0.02
decay_rate = 0.1
epsilon = 1e-08
clip_level = 0.5
bias_one = 1.0 - 0.9**20
bias_two = 1.0 - 0.95**20
average_decay = 0.99


def clip_factor(square_sum):
    entries = LAYERS * (D * IN_COLS + OUT_ROWS * D + NORM_LEN) + VOCAB_ROWS * D
    return jnp.minimum(1.0, clip_level * math.sqrt(entries) / (jnp.sqrt(square_sum) + 1e-06))


def adam_update(gradient, momentum, variance, master, clip_scale):
    clipped = clip_scale * gradient
    moved_first = beta_one * momentum + (1.0 - beta_one) * clipped
    moved_second = beta_two * variance + (1.0 - beta_two) * clipped * clipped
    stepped = master * (1.0 - learn_rate * decay_rate) - learn_rate * (moved_first / bias_one) / (
        jnp.sqrt(moved_second / bias_two) + epsilon
    )
    return (stepped, moved_first, moved_second)


LANES = 128
TILE_ROWS = 640


def swap(moving, axis, distance):
    count = lax.axis_size(axis)
    return lax.ppermute(moving, axis, [(i, i ^ distance) for i in range(count)])


def all_sum(value, axis):
    count = lax.axis_size(axis)
    step = 1
    while step < count:
        if step * 2 < count:
            one = swap(value, axis, step)
            two = swap(value, axis, step * 2)
            three = swap(value, axis, step * 3)
            value = (value + one) + (two + three)
            step = step * 4
        else:
            value = value + swap(value, axis, step)
            step = step * 2
    return value


def after(value, *earlier):
    return lax.optimization_barrier((value, *earlier))[0]


def halves(matrix_block):
    half = matrix_block.shape[1] // lax.axis_size("rep")
    mine = lax.axis_index("rep")
    kept = lax.dynamic_slice_in_dim(matrix_block, mine * half, half, 1)
    sent = lax.dynamic_slice_in_dim(matrix_block, (1 - mine) * half, half, 1)
    return kept, swap(sent, "rep", 1)


def half_sum(kept, arrived):
    total = (kept.astype(jnp.float32) + arrived.astype(jnp.float32)).astype(jnp.bfloat16)
    return total, jnp.sum(jnp.square(total.astype(jnp.float32)))


def thin_body(kept_ref, arrived_ref, *refs):
    pieces_ref, squares_ref = refs[-2:]
    row_count, chunks, width, lanes = pieces_ref.shape
    total = kept_ref[0].astype(jnp.float32) + arrived_ref[0].astype(jnp.float32)
    total = total.astype(jnp.bfloat16).astype(jnp.float32)
    squares_ref[0] = jnp.sum(total * total, axis=0, keepdims=True)
    for r in range(row_count):
        for c in range(chunks):
            piece = total[r * width : (r + 1) * width, c * lanes : (c + 1) * lanes]
            pieces_ref[r, c] = piece.astype(jnp.bfloat16)


def thin_sum(kept, arrived, row_count, lanes, count, start, carried):
    layer_count, half, block_cols = kept.shape
    chunks = half // lanes
    first = start // chunks
    whole = pl.BlockSpec((1, block_cols, half), lambda i: (i, 0, 0))
    width = block_cols // row_count
    extra = [] if carried is None else [carried]
    pieces, squares = pl.pallas_call(
        thin_body,
        grid=(layer_count,),
        in_specs=[whole, whole] + [pl.BlockSpec(memory_space=pl.ANY) for _ in extra],
        out_specs=[
            pl.BlockSpec((row_count, chunks, width, lanes), lambda i: (0, i + first, 0, 0)),
            pl.BlockSpec((1, 1, half), lambda i: (i, 0, 0)),
        ],
        out_shape=[
            jax.ShapeDtypeStruct((row_count, count, width, lanes), jnp.bfloat16),
            jax.ShapeDtypeStruct((layer_count, 1, half), jnp.float32),
        ],
        input_output_aliases={2 + k: k for k in range(len(extra))},
        name="thin_sum",
    )(kept.transpose(0, 2, 1), arrived.transpose(0, 2, 1), *extra)
    return pieces, jnp.sum(squares)


def thin_join(exit_pair, embed_pair, row_count):
    counts = []
    lanes = math.gcd(exit_pair[0].shape[1], embed_pair[0].shape[1])
    for kept, _ in (exit_pair, embed_pair):
        counts.append(kept.shape[0] * kept.shape[1] // lanes)
    embed_chunks = embed_pair[0].shape[1] // lanes
    width = embed_pair[0].shape[2] // row_count
    if lanes % LANES == 0 and width % 8 == 0 and counts[0] % embed_chunks == 0:
        joined, one = thin_sum(*exit_pair, row_count, lanes, sum(counts), 0, None)
        joined, two = thin_sum(*embed_pair, row_count, lanes, sum(counts), counts[0], joined)
        return joined, one + two, counts[0]
    exit_total, one = half_sum(*exit_pair)
    embed_total, two = half_sum(*embed_pair)
    thin = [thin_pieces(part, row_count, lanes) for part in (exit_total, embed_total)]
    return jnp.concatenate(thin, axis=1), one + two, counts[0]


def both_halves(half):
    other = swap(half, "rep", 1)
    first = lax.axis_index("rep") == 0
    return jnp.concatenate(
        [jnp.where(first, half, other), jnp.where(first, other, half)], axis=1
    )


def move(pieces):
    return lax.all_to_all(pieces, "row", split_axis=0, concat_axis=0, tiled=True)


def owner_pieces(part, row_count):
    layer_count, half, block_cols = part.shape
    return part.reshape(layer_count, half, row_count, -1).transpose(2, 0, 1, 3)


def thin_pieces(part, row_count, lanes):
    layer_count, half, block_cols = part.shape
    split = part.reshape(layer_count, half // lanes, lanes, row_count, -1)
    return split.transpose(3, 0, 1, 4, 2).reshape(row_count, -1, split.shape[4], lanes)


def thin_rows(arrived, part):
    row_count, _, width, lanes = arrived.shape
    split = arrived.reshape(row_count, part.shape[0], -1, width, lanes)
    return split.transpose(1, 0, 2, 4, 3).reshape(-1, LANES)


def holder_pieces(section, narrow):
    if narrow:
        return section.transpose(1, 0, 3, 2)
    return section.transpose(1, 0, 2, 3)


def holder_block(arrived, narrow):
    if narrow:
        block = arrived.transpose(1, 3, 0, 2)
    else:
        block = arrived.transpose(1, 2, 0, 3)
    return block.reshape(*block.shape[:2], -1)


def update_body(scale_ref, gradient_ref, momentum_ref, variance_ref, master_ref, *refs):
    master_out, momentum_out, variance_out, weight_out = refs[-4:]
    stepped, moved_first, moved_second = adam_update(
        gradient_ref[...].astype(jnp.float32),
        momentum_ref[...],
        variance_ref[...],
        master_ref[...],
        scale_ref[0, 0],
    )
    master_out[...] = stepped
    momentum_out[...] = moved_first
    variance_out[...] = moved_second
    weight_out[...] = stepped.astype(jnp.bfloat16)


def update_section(scale, gradient, momentum, variance, master, start, carried):
    rows = gradient.shape[0]
    tile = math.gcd(math.gcd(rows, start), TILE_ROWS)
    first = start // tile
    here = pl.BlockSpec((tile, LANES), lambda i: (i, 0))
    there = pl.BlockSpec((tile, LANES), lambda i: (i + first, 0))
    whole = jax.ShapeDtypeStruct(master.shape, jnp.float32)
    extra = [] if carried is None else list(carried)
    return pl.pallas_call(
        update_body,
        grid=(rows // tile,),
        in_specs=[pl.BlockSpec(memory_space=pltpu.SMEM), here, there, there, there]
        + [pl.BlockSpec(memory_space=pl.ANY) for _ in extra],
        out_specs=[there, there, there, here],
        out_shape=[whole, whole, whole, jax.ShapeDtypeStruct(gradient.shape, jnp.bfloat16)],
        input_output_aliases={5 + k: k for k in range(len(extra))},
        name="update",
    )(scale, gradient, momentum, variance, master, *extra)


def shards(
    entry_gradient,
    exit_gradient,
    embed_gradient,
    gain_gradient,
    master,
    momentum,
    variance,
    entry_average,
    exit_average,
    embed_average,
    gain_master,
    gain_momentum,
    gain_variance,
):
    row_count = lax.axis_size("row")
    matrices = [entry_gradient[0], exit_gradient[0], embed_gradient[0][None]]
    averages = [entry_average, exit_average, embed_average[None]]
    gain_local = gain_gradient[0]
    gain_total = gain_local.astype(jnp.float32) + swap(gain_local, "rep", 1).astype(jnp.float32)
    gain_total = gain_total.astype(jnp.bfloat16).astype(jnp.float32)
    pairs = [halves(matrix_block) for matrix_block in matrices]
    thin, local_squares, split = thin_join(pairs[1], pairs[2], row_count)
    entry_total, entry_squares = half_sum(*pairs[0])
    local_squares = (local_squares + entry_squares).reshape(1, 1)
    row_squares = all_sum(all_sum(local_squares, "rep"), "row")
    clip_scale = clip_factor(all_sum(row_squares, "tp") + jnp.sum(gain_total * gain_total))

    flat = [array.reshape(-1, LANES) for array in (momentum, variance, master)]
    parts = [kept for kept, _ in pairs]
    starts = [0, parts[0].size // LANES, (parts[0].size + parts[1].size) // LANES]
    narrow = [part.shape[2] < part.shape[1] for part in parts]
    thin_moved = move(thin)
    entry_moved = move(after(owner_pieces(entry_total, row_count), thin_moved, row_squares))
    thin_arrived = after(thin_moved, clip_scale)
    rows = [
        entry_moved.transpose(1, 0, 2, 3).reshape(-1, LANES),
        thin_rows(thin_arrived[:, :split], parts[1]),
        thin_rows(thin_arrived[:, split:], parts[2]),
    ]
    carried = None
    pieces = [None] * 3
    for k in (2, 1, 0):
        layer_count, half, block_cols = parts[k].shape
        *carried, weight = update_section(clip_scale, rows[k], *flat, starts[k], carried)
        pieces[k] = holder_pieces(
            weight.reshape(layer_count, row_count, half, block_cols // row_count), narrow[k]
        )
    back = [None] * 3
    weights = [None] * 3
    averaged = [None] * 3

    def settle(k):
        weights[k] = both_halves(holder_block(back[k], narrow[k]))
        averaged[k] = average_decay * averages[k] + (1.0 - average_decay) * weights[k].astype(
            jnp.float32
        )

    back[1] = move(after(pieces[1], entry_moved))
    settle(1)
    back[0] = move(after(pieces[0], back[1]))
    back[2] = move(after(pieces[2], back[0], averaged[1]))
    settle(0)
    settle(2)
    fresh_gain, fresh_momentum, fresh_variance = adam_update(
        gain_total, gain_momentum, gain_variance, gain_master, clip_scale
    )
    next_master, next_momentum, next_variance = [array.reshape(master.shape) for array in carried]
    return (
        next_master,
        next_momentum,
        next_variance,
        weights[0],
        weights[1],
        weights[2][0],
        averaged[0],
        averaged[1],
        averaged[2][0],
        fresh_gain,
        fresh_momentum,
        fresh_variance,
    )


def solution(mesh):
    placed = (
        P("rep", None, "row", "tp"),
        P("rep", None, "row", "tp"),
        P("rep", "row", "tp"),
        P("rep", None, None),
        P("tp", "row", "rep", None),
        P("tp", "row", "rep", None),
        P("tp", "row", "rep", None),
        P(None, "row", "tp"),
        P(None, "row", "tp"),
        P("row", "tp"),
        P(),
        P(),
        P(),
    )
    return jax.shard_map(
        shards,
        mesh=mesh,
        in_specs=placed,
        out_specs=(
            P("tp", "row", "rep", None),
            P("tp", "row", "rep", None),
            P("tp", "row", "rep", None),
            P(None, "row", "tp"),
            P(None, "row", "tp"),
            P("row", "tp"),
            P(None, "row", "tp"),
            P(None, "row", "tp"),
            P("row", "tp"),
            P(),
            P(),
            P(),
        ),
        check_vma=False,
    )
```
